256 devices in a mesh: seq: 64 (over x, z, core), head: 4 (over y).
Axes of the slice: x: 4, y: 4, z: 8, core: 2. Of those that a mesh axis runs over, the one named last changes fastest.
Arguments:
- tokens: bfloat16 [21504, 4096], P('seq', 'head')
- w_short: float32 [3, 4096], P(None, 'head'), may hold values from 0.25 to 1.5
- w_query: bfloat16 [4096, 2048], P(None, 'head')
- w_key: bfloat16 [4096, 2048], P(None, 'head')
- w_value: bfloat16 [4096, 2048], P(None, 'head'), may hold values from -0.09375 to 0.09375
- owner_lengths: int32 [64], replicated, may hold values from 1 to 224, as said below
Outputs:
- attended: bfloat16 [14336, 2048], P('seq', 'head')
The draws below stay inside these ranges and needn't reach their ends.
Inputs may be any that keep to these rules, and one draw needn't show every extreme that they name: The counts sum to 7168; owner o holds the coarse rows from starts[o] on, with o * 112 <= starts[o] and starts[o] + owner_lengths[o] <= (o + 2) * 112; the largest count is exactly 224.
All inputs are finite; a program needn't handle non-finite values.
Results may differ from the reference program's by a relative error of at most 0.012.
The reference program's roundings to bfloat16 on the way count: a program that leaves them out, or rounds other values in their place, can miss the bound.
Values may be sent and summed in bfloat16 or wider, within the bound.
A program may use at most 128 MiB of HBM per device.

```python
import math
import jax
import jax.numpy as jnp
from jax import lax

D = 4096
HD = 128
STRIDE = 3
HEADS = 16
TOKENS = 21504
CD = 112
COARSE = 7168
CAP = 224
N_SEQ = 64


def common_projection(key):
    return jax.random.normal(jax.random.fold_in(key, 7), (D, HEADS * HD), jnp.float32) * D ** (-0.5)


def draw_tokens(key, part):
    noise_key, column_key = jax.random.split(key, 2)
    columns = 3.0 ** (jnp.arange(D, dtype=jnp.float32) / D) * jax.random.uniform(column_key, (D,), jnp.float32, 0.7, 1.4)
    values = jax.random.normal(noise_key, (TOKENS, D), jnp.float32) * columns[None, :]
    return values.astype(jnp.bfloat16)


def draw_w_query(key, part):
    return (3.0 * common_projection(key)).astype(jnp.bfloat16)


def draw_w_key(key, part):
    separate = jax.random.normal(jax.random.fold_in(key, 8), (D, HEADS * HD), jnp.float32) * D ** (-0.5)
    values = separate
    return values.astype(jnp.bfloat16)


def draw_owner_lengths(key, part):
    middle = jax.random.randint(jax.random.fold_in(key, 11), (N_SEQ - 2,), 1, CD)
    drift = jnp.concatenate([jnp.zeros((1,), jnp.int32), jnp.full((1,), CD, jnp.int32), middle.astype(jnp.int32), jnp.zeros((1,), jnp.int32)])
    return (CD + drift[1:] - drift[:-1]).astype(jnp.int32)


def block_scale(rng, dims, shards, least, top_value):
    level = 1.0
    for dim, parts in shards:
        heights = jax.random.uniform(jax.random.fold_in(jax.random.fold_in(rng, 6), dim), (parts,), jnp.float32, least / len(shards), top_value / len(shards))
        level = level * jnp.repeat(jnp.exp(heights), dims[dim] // parts).reshape((-1,) + (1,) * (len(dims) - 1 - dim))
    return level


def bell_draw(key, dims, spread, limit, pieces=(), kind=jnp.bfloat16):
    entries = spread * jax.random.normal(key, dims, jnp.float32)
    if pieces:
        entries = entries * block_scale(key, dims, pieces, -0.22, 0.18)
    return jnp.clip(entries, -limit, limit).astype(kind)


def setup_inputs(seed: int = 0) -> dict:
    key_list = jax.random.split(jax.random.key(seed), 7)
    tokens = draw_tokens(jax.random.fold_in(key_list[6], 71), 0)
    w_short = jnp.clip(0.25 + 1.25 * jax.random.uniform(key_list[1], (STRIDE, D), jnp.float32) ** block_scale(key_list[1], (STRIDE, D), ((1, 4),), -0.2, 0.2), 0.25, 1.5)
    w_query = draw_w_query(jax.random.fold_in(key_list[6], 71), 0)
    w_key = draw_w_key(jax.random.fold_in(key_list[6], 71), 0)
    w_value = bell_draw(key_list[4], (D, HEADS * HD), D ** -0.5, 0.09375, ((1, 4),))
    owner_lengths = draw_owner_lengths(jax.random.fold_in(key_list[6], 71), 0)
    return dict(tokens=tokens, w_short=w_short, w_query=w_query, w_key=w_key, w_value=w_value, owner_lengths=owner_lengths)


def reference(tokens, w_short, w_query, w_key, w_value, owner_lengths):
    shifted = jnp.concatenate([jnp.zeros((2, D), tokens.dtype), tokens[:TOKENS - 2]], axis=0)
    grouped = shifted.reshape(COARSE, 3, D)
    pooled = grouped[:, 0].astype(jnp.float32) * w_short[0] + grouped[:, 1].astype(jnp.float32) * w_short[1] + grouped[:, 2].astype(jnp.float32) * w_short[2]
    norm_scale = lax.rsqrt(lax.optimization_barrier(jnp.mean(pooled * pooled, axis=1, keepdims=True)) + 1e-05)
    coarse = (pooled * norm_scale).astype(jnp.bfloat16)
    queries = jnp.dot(coarse, w_query, preferred_element_type=jnp.float32).astype(jnp.bfloat16)
    key_rows = jnp.dot(coarse, w_key, preferred_element_type=jnp.float32).astype(jnp.bfloat16)
    value_rows = jnp.dot(coarse, w_value, preferred_element_type=jnp.float32).astype(jnp.bfloat16)
    inverse = 1.0 / math.sqrt(HD)
    positions = jnp.arange(COARSE, dtype=jnp.int32)
    allowed = positions[None, :] <= positions[:, None]

    def heads_first(matrix):
        return matrix.reshape(COARSE, HEADS, HD).transpose(1, 0, 2)

    def one_head(operands):
        query_head, key_head, value_head = operands
        scores = jnp.dot(query_head, key_head.T, preferred_element_type=jnp.float32) * inverse
        scores = jnp.where(allowed, scores, -1e+30)
        maxima = lax.optimization_barrier(jnp.max(scores, axis=1, keepdims=True))
        weights = jnp.exp(scores - maxima)
        totals = lax.optimization_barrier(jnp.sum(weights, axis=1, keepdims=True))
        return jnp.dot(weights.astype(jnp.bfloat16), value_head, preferred_element_type=jnp.float32) / totals
    context = lax.map(one_head, (heads_first(queries), heads_first(key_rows), heads_first(value_rows)))
    merged = context.transpose(1, 0, 2).reshape(COARSE, HEADS * HD)
    lengths = owner_lengths.astype(jnp.int32)
    starts = (jnp.cumsum(lengths) - lengths).astype(jnp.int32)
    slots = jnp.arange(CAP, dtype=jnp.int32)
    wanted = (starts[:, None] + slots[None, :]).astype(jnp.int32)
    live = slots[None, :] < lengths[:, None]
    gathered = jnp.take(merged, jnp.clip(wanted, 0, COARSE - 1).reshape(-1), axis=0)
    return jnp.where(live.reshape(-1, 1), gathered, 0.0).astype(jnp.bfloat16)
```

```python
import functools
import math

import jax
import jax.numpy as jnp
from jax import lax
from jax.experimental import pallas as pl
from jax.experimental.pallas import tpu as pltpu
from jax.sharding import PartitionSpec as P

HD = 128
NX = 4
NY = 4
MASKED = -1e30
F32 = jnp.float32
BF16 = jnp.bfloat16
DORDER = (0, 1, 3, 2)


def layer_kernel(
    seqs, width,
    tokens, w_short, w_q, w_k, w_v, lengths,
    out,
    tok, tok32, pooled, part, sums, coarse, weights, acc, kv_out, q_out, kv, q_all,
    m_s, l_s, o_s, ctx, win,
    tok_sem, w_sem, bnd_sem, ss_send, ss_recv, y_send, y_recv,
    s2_send, s2_recv, q_send, q_recv, cw_send, cw_recv, ccw_send, ccw_recv,
    pt_send, pt_recv, o_send, o_recv, n_send, n_recv,
):
    NZ = seqs // (2 * NX)
    NT = NZ // 2
    NZC = 2 * NZ
    rows, part_width = tok.shape
    CD = rows // 3
    lane_blocks = part_width // 128
    half = part_width // 2
    features = NX * HD

    s = lax.axis_index("seq")
    y = lax.axis_index("head")
    x = s // NZC
    zc = s % NZC
    z = zc // 2
    c = zc % 2

    def seq_id(xx, zz, cc):
        return (xx * NZ + zz) * 2 + cc

    def at_seq(i):
        return (i, y)

    def remote(src, dst, send, recv, device):
        return pltpu.make_async_remote_copy(
            src_ref=src, dst_ref=dst, send_sem=send, recv_sem=recv,
            device_id=device, device_id_type=pl.DeviceIdType.MESH,
        )

    z_up = seq_id(x, (z + 1) % NZ, c)
    z_down = seq_id(x, (z + NZ - 1) % NZ, c)
    partner = seq_id(x, z, 1 - c)

    def x_peer(d):
        return ((x + d) % NX) * NZC + zc

    barrier = pltpu.get_barrier_semaphore()
    greeted = [((s + seqs - 1) % seqs, y)]
    greeted += [(s, (y + d) % NY) for d in (1, 2, 3)]
    greeted += [(x_peer(d), y) for d in (1, 2, 3)]
    greeted += [(z_up, y), (z_down, y), (partner, y)]
    greeted += [(((x + d) % NX) * NZC + (zc + 1) % NZC, y) for d in range(NX)]
    for device in greeted:
        pl.semaphore_signal(barrier, inc=1, device_id=device, device_id_type=pl.DeviceIdType.MESH)

    tail = 16
    tail_copy = pltpu.make_async_copy(
        tokens.at[pl.ds(rows - tail, tail)], tok.at[pl.ds(rows - tail, tail)], tok_sem.at[0])
    head_copy = pltpu.make_async_copy(
        tokens.at[pl.ds(0, rows - tail)], tok.at[pl.ds(0, rows - tail)], tok_sem.at[1])
    tail_copy.start()
    head_copy.start()
    y_of_slot = [y, (y + 3) % NY, (y + 1) % NY, (y + 2) % NY]
    w_copies = []
    for slot in range(4):
        for j, w in enumerate((w_k, w_v, w_q)):
            rows_w = pl.ds(pl.multiple_of(y_of_slot[slot] * part_width, part_width), part_width)
            cp = pltpu.make_async_copy(w.at[rows_w], weights.at[slot, j], w_sem.at[slot, j])
            cp.start()
            w_copies.append(cp)

    tail_copy.wait()
    for b in range(lane_blocks):
        tok32[b, pl.ds(rows - 8, 16), :] = tok[pl.ds(rows - tail, tail), pl.ds(b * 128, 128)].astype(F32)
    pl.semaphore_wait(barrier, len(greeted))
    bnd = remote(
        tok32.at[:, pl.ds(rows, 8), :], tok32.at[:, pl.ds(0, 8), :],
        bnd_sem.at[0], bnd_sem.at[1], at_seq((s + 1) % seqs))
    bnd.start()
    head_copy.wait()
    for b in range(lane_blocks):
        tok32[b, pl.ds(8, rows - tail), :] = tok[pl.ds(0, rows - tail), pl.ds(b * 128, 128)].astype(F32)
    bnd.wait_recv()

    @pl.when(s == 0)
    def _():
        tok32[:, pl.ds(0, 8), :] = jnp.zeros((lane_blocks, 8, 128), F32)

    part[...] = jnp.zeros_like(part)
    square = jnp.zeros((CD, 128), F32)
    for b in range(lane_blocks):
        lanes = pl.ds(b * 128, 128)
        first = tok32[b, pl.ds(6, CD, stride=3), :]
        second = tok32[b, pl.ds(7, CD, stride=3), :]
        third = tok32[b, pl.ds(8, CD, stride=3), :]
        p = first * w_short[0:1, lanes] + second * w_short[1:2, lanes] + third * w_short[2:3, lanes]
        pooled[b] = p
        square = square + p * p
    part[pl.ds(0, CD), :] = square
    sums[0] = jnp.broadcast_to(jnp.sum(part[...].T, axis=0, keepdims=True), (8, 128))
    ss = []
    for d in (1, 2, 3):
        cp = remote(sums.at[0], sums.at[d], ss_send.at[d - 1], ss_recv.at[d - 1], (s, (y + d) % NY))
        cp.start()
        ss.append(cp)
    for cp in ss:
        cp.wait_recv()
    total = sums[0] + sums[1] + sums[2] + sums[3]
    scale_row = lax.rsqrt(total / width + 1e-05)
    part[...] = jnp.broadcast_to(scale_row[0:1], (128, 128))
    scale = part[...].T[0:CD]
    for b in range(lane_blocks):
        h, o = divmod(b * 128, half)
        coarse[0, h, :, pl.ds(o, 128)] = (pooled[b] * scale).astype(BF16)

    y_up = (s, (y + 1) % NY)
    y_down = (s, (y + 3) % NY)
    sends = []

    def y_copy(src, dst, h, i, device):
        r = (dst - 1) * 2 + h
        return remote(coarse.at[src, h], coarse.at[dst, h], y_send.at[i], y_recv.at[r], device)

    own = [y_copy(0, 1, 0, 0, y_up), y_copy(0, 2, 1, 1, y_down), y_copy(0, 1, 1, 2, y_up), y_copy(0, 2, 0, 3, y_down)]
    for cp in own:
        cp.start()
        sends.append(cp)
    relay = [y_copy(1, 3, 0, 4, y_up), y_copy(2, 3, 1, 5, y_down)]

    def wait_block(slot, h):
        y_copy(slot, slot, h, 0, y_up).wait_recv()

    def project(slot, h, j):
        w = weights[slot, j, pl.ds(h * half, half), :]
        return jnp.dot(coarse[slot, h], w, preferred_element_type=F32)

    def add_block(slot, h):
        for j in range(3):
            acc[j] = acc[j] + project(slot, h, j)

    for j in range(3):
        w_copies[j].wait()
        acc[j] = jnp.dot(coarse[0, 0], weights[0, j, pl.ds(0, half), :], preferred_element_type=F32)
    wait_block(1, 0)
    relay[0].start()
    wait_block(2, 1)
    relay[1].start()
    sends += relay
    add_block(0, 1)
    for cp in w_copies[3:]:
        cp.wait()
    add_block(1, 0)
    add_block(2, 1)
    wait_block(1, 1)
    add_block(1, 1)
    wait_block(2, 0)
    add_block(2, 0)
    wait_block(3, 0)
    add_block(3, 0)
    wait_block(3, 1)

    def x_abs(d):
        return (x + d) % NX

    def block_rows(xx):
        return pl.ds(pl.multiple_of(xx * CD, CD), CD)

    def sub(slot, d):
        return kv.at[slot, :, block_rows(x_abs(d)), :]

    for j in range(2):
        r = (acc[j] + project(3, 1, j)).astype(BF16)
        for h in range(NX):
            kv_out[h, j] = r[:, h * HD:(h + 1) * HD]
    for d in (1, 3, 2):
        cp = remote(
            kv_out.at[x_abs(d)], kv.at[0, :, block_rows(x), :],
            s2_send.at[d - 1], s2_recv.at[NX - d - 1], at_seq(x_peer(d)))
        cp.start()
        sends.append(cp)
    own_kv = kv_out[x]
    kv[0, :, block_rows(x), :] = own_kv

    def ring_copy(up, src_slot, t_next, dst_slot, i, d):
        send = cw_send if up else ccw_send
        recv = cw_recv if up else ccw_recv
        return remote(
            sub(src_slot, d), sub(dst_slot, d), send.at[t_next - 1, i], recv.at[t_next - 1, i],
            at_seq(z_up if up else z_down))

    def partner_copy(slot, i, d):
        return remote(sub(slot, d), sub(NZ + slot, d), pt_send.at[slot, i], pt_recv.at[slot, i], at_seq(partner))

    last = NZ - 1

    def start_ring(i, d):
        for up in (True, False):
            if NT > 1:
                ring_copy(up, 0, 1, 1 if up else NT, i, d).start()
            elif (i < 2) == up:
                ring_copy(up, 0, 1, last, i, d).start()
        partner_copy(0, i, d).start()

    start_ring(0, 0)

    r = (acc[2] + project(3, 1, 2)).astype(BF16)
    for h in range(NX):
        q_out[h] = r[:, h * HD:(h + 1) * HD]
    for d in (1, 3, 2):
        cp = remote(
            q_out.at[x_abs(d)], q_all.at[x], q_send.at[d - 1], q_recv.at[NX - d - 1], at_seq(x_peer(d)))
        cp.start()
        sends.append(cp)
    q_all[x] = q_out[x]

    for i, d in enumerate(DORDER):
        if d:
            remote(sub(0, d), sub(0, d), s2_send.at[0], s2_recv.at[d - 1], at_seq(partner)).wait_recv()
            start_ring(i, d)
    for d in (1, 3, 2):
        remote(q_all.at[x_abs(d)], q_all.at[x_abs(d)], q_send.at[0], q_recv.at[d - 1], at_seq(partner)).wait_recv()

    inverse = 1.0 / math.sqrt(HD)

    def attend(slot, allowed, first=False):
        for xq in range(NX):
            nk = (xq + 1) * CD
            keys = kv[slot, 0, pl.ds(0, nk), :]
            values = kv[slot, 1, pl.ds(0, nk), :]
            sc = lax.dot_general(q_all[xq], keys, (((1,), (1,)), ((), ())), preferred_element_type=F32) * inverse
            column = lax.broadcasted_iota(jnp.int32, (CD, nk), 1)
            if first:
                limit = lax.broadcasted_iota(jnp.int32, (CD, nk), 0) + (xq * CD + 1)
            else:
                limit = jnp.where(allowed, nk, xq * CD)
            sc = jnp.where(column < limit, sc, MASKED)
            top = jnp.max(sc, axis=1, keepdims=True)
            if not first:
                old = m_s[xq]
                new = jnp.maximum(old, top)
                alpha = jnp.exp(old - new)
                m_s[xq] = new
                top = new[:, 0:1]
            else:
                m_s[xq] = jnp.broadcast_to(top, (CD, HD))
            w = jnp.exp(sc - top)
            added = jnp.dot(w.astype(BF16), values, preferred_element_type=F32)
            lw = jnp.sum(w, axis=1, keepdims=True)
            if first:
                l_s[xq] = jnp.broadcast_to(lw, (CD, HD))
                o_s[xq] = added
            else:
                l_s[xq] = l_s[xq] * alpha + lw
                o_s[xq] = o_s[xq] * alpha + added

    def wait_partner(slot):
        for i, d in enumerate(DORDER):
            remote(sub(NZ + slot, d), sub(NZ + slot, d), pt_send.at[slot, i], pt_recv.at[slot, i], at_seq(partner)).wait_recv()

    attend(0, None, first=True)
    wait_partner(0)
    attend(NZ, c == 1)

    def arrived(up, t, slot, i, d):
        recv = cw_recv if up else ccw_recv
        send = cw_send if up else ccw_send
        remote(sub(slot, d), sub(slot, d), send.at[t - 1, i], recv.at[t - 1, i], at_seq(partner)).wait_recv()

    def ring_step(t, carry):
        for i, d in enumerate(DORDER):
            for up in (True, False):
                slot = t if up else NT - 1 + t
                arrived(up, t, slot, i, d)

                @pl.when(t + 1 < NT)
                def _():
                    ring_copy(up, slot, t + 1, slot + 1, i, d).start()

                if (i < 2) == up:
                    @pl.when(t + 1 == NT)
                    def _():
                        ring_copy(up, slot, t + 1, last, i, d).start()

                partner_copy(slot, i, d).start()

        def both(k, carry):
            @pl.when(k >= 2)
            def _():
                wait_partner(t + (k % 2) * (NT - 1))

            slot = t + (k % 2) * (NT - 1) + (k // 2) * NZ
            lower = jnp.where(k % 2 == 0, z - t, z + t - NZ) >= 0
            attend(slot, lower)
            return carry

        lax.fori_loop(0, 4, both, 0)
        return carry

    lax.fori_loop(1, NT, ring_step, 0)

    for i, d in enumerate(DORDER):
        arrived(i < 2, NT, last, i, d)
        partner_copy(last, i, d).start()
    lower = z >= NT
    attend(last, lower)
    wait_partner(last)
    attend(NZ + last, lower)

    for xq in range(NX):
        ctx[xq] = (o_s[xq] / l_s[xq]).astype(BF16)
    wrap = jnp.where(zc == 0, 1, 0)
    before = (zc + NZC - 1) % NZC
    for d in (1, 3, 2):
        cp = remote(
            ctx.at[x_abs(d)], win.at[x, pl.ds(0, CD), :], o_send.at[d - 1], o_recv.at[NX - d - 1], at_seq(x_peer(d)))
        cp.start()
        sends.append(cp)
    for d in DORDER:
        target = x_abs(d) * NZC + before
        cp = remote(
            ctx.at[(x + d + wrap) % NX], win.at[x, pl.ds(CD, CD), :], n_send.at[d], n_recv.at[(NX - d) % NX], at_seq(target))
        cp.start()
        sends.append(cp)
    win[x, pl.ds(0, CD), :] = ctx[x]
    for d in (1, 3, 2):
        dst = win.at[x_abs(d), pl.ds(0, CD), :]
        remote(dst, dst, o_send.at[0], o_recv.at[d - 1], at_seq(partner)).wait_recv()
    for d in DORDER:
        dst = win.at[x_abs(d), pl.ds(CD, CD), :]
        remote(dst, dst, n_send.at[0], n_recv.at[d], at_seq(partner)).wait_recv()

    lane = lax.broadcasted_iota(jnp.int32, (1, seqs), 1)
    lens = lengths[...]
    start = jnp.sum(jnp.where(lane < s, lens, 0), axis=1, keepdims=True) - s * CD
    count = jnp.sum(jnp.where(lane == s, lens, 0), axis=1, keepdims=True)
    row = lax.broadcasted_iota(jnp.int32, (2 * CD, 2 * CD), 0)
    col = lax.broadcasted_iota(jnp.int32, (2 * CD, 2 * CD), 1)
    pick = jnp.where((col == row + start) & (row < count), 1.0, 0.0).astype(BF16)
    for h in range(NX):
        out[:, pl.ds(h * HD, HD)] = jnp.dot(pick, win[h], preferred_element_type=F32).astype(BF16)

    bnd.wait_send()
    for cp in ss + sends:
        cp.wait_send()
    for i, d in enumerate(DORDER):
        def sent(t, carry):
            for up in (True, False):
                ring_copy(up, 0, t, 0, i, d).wait_send()
            return carry

        lax.fori_loop(1, NT, sent, 0)
        ring_copy(i < 2, 0, NT, 0, i, d).wait_send()

        def passed(slot, carry):
            partner_copy(slot, i, d).wait_send()
            return carry

        lax.fori_loop(0, NZ, passed, 0)


def shards(seqs, tokens, w_short, w_query, w_key, w_value, owner_lengths):
    rows, part_width = tokens.shape
    CD = rows // 3
    width = part_width * NY
    features = w_query.shape[1]
    NZ = seqs // (2 * NX)
    NT = NZ // 2
    half = part_width // 2
    dma = pltpu.SemaphoreType.DMA
    vmem = pl.BlockSpec(memory_space=pltpu.VMEM)
    hbm = pl.BlockSpec(memory_space=pl.ANY)
    return pl.pallas_call(
        functools.partial(layer_kernel, seqs, width),
        out_shape=jax.ShapeDtypeStruct((2 * CD, features), BF16),
        in_specs=[hbm, vmem, hbm, hbm, hbm, vmem],
        out_specs=vmem,
        scratch_shapes=[
            pltpu.VMEM((rows, part_width), BF16),
            pltpu.VMEM((part_width // 128, rows + 8, 128), F32),
            pltpu.VMEM((part_width // 128, CD, 128), F32),
            pltpu.VMEM((128, 128), F32),
            pltpu.VMEM((4, 8, 128), F32),
            pltpu.VMEM((4, 2, CD, half), BF16),
            pltpu.VMEM((4, 3, part_width, features), BF16),
            pltpu.VMEM((3, CD, features), F32),
            pltpu.VMEM((NX, 2, CD, HD), BF16),
            pltpu.VMEM((NX, CD, HD), BF16),
            pltpu.VMEM((2 * NZ, 2, NX * CD, HD), BF16),
            pltpu.VMEM((NX, CD, HD), BF16),
            pltpu.VMEM((NX, CD, HD), F32),
            pltpu.VMEM((NX, CD, HD), F32),
            pltpu.VMEM((NX, CD, HD), F32),
            pltpu.VMEM((NX, CD, HD), BF16),
            pltpu.VMEM((NX, 2 * CD, HD), BF16),
            dma((2,)), dma((4, 3)), dma((2,)), dma((3,)), dma((3,)), dma((6,)), dma((6,)),
            dma((3,)), dma((3,)), dma((3,)), dma((3,)),
            dma((NT, 4)), dma((NT, 4)), dma((NT, 4)), dma((NT, 4)),
            dma((NZ, 4)), dma((NZ, 4)), dma((3,)), dma((3,)), dma((4,)), dma((4,)),
        ],
        compiler_params=pltpu.CompilerParams(
            collective_id=0, has_side_effects=True, vmem_limit_bytes=56 * 1024 * 1024),
        name="layer",
    )(tokens, w_short, w_query, w_key, w_value, owner_lengths.reshape(1, seqs))


def solution(mesh):
    return jax.shard_map(
        functools.partial(shards, mesh.shape["seq"]),
        mesh=mesh,
        in_specs=(
            P("seq", "head"),
            P(None, "head"),
            P(None, "head"),
            P(None, "head"),
            P(None, "head"),
            P(),
        ),
        out_specs=P("seq", "head"),
        check_vma=False,
    )
```

```python
import functools
import math

import jax
import jax.numpy as jnp
from jax import lax
from jax.experimental import pallas as pl
from jax.experimental.pallas import tpu as pltpu
from jax.sharding import PartitionSpec as P

HD = 128
NX = 4
NY = 4
MASKED = -1e30
F32 = jnp.float32
BF16 = jnp.bfloat16
DORDER = (0, 1, 3, 2)


def layer_kernel(
    seqs, width,
    tokens, w_short, w_q, w_k, w_v, lengths,
    out,
    tok, tok32, pooled, part, sums, coarse, weights, acc, kv_out, q_out, kv, q_all,
    q_t, m_s, l_s, o_s, ctx, win,
    tok_sem, w_sem, bnd_sem, ss_send, ss_recv, y_send, y_recv,
    s2_send, s2_recv, q_send, q_recv, cw_send, cw_recv, ccw_send, ccw_recv,
    pt_send, pt_recv, o_send, o_recv, n_send, n_recv,
):
    NZ = seqs // (2 * NX)
    NT = NZ // 2
    NZC = 2 * NZ
    rows, part_width = tok.shape
    CD = rows // 3
    lane_blocks = part_width // 128
    half = part_width // 2
    features = NX * HD

    s = lax.axis_index("seq")
    y = lax.axis_index("head")
    x = s // NZC
    zc = s % NZC
    z = zc // 2
    c = zc % 2

    def seq_id(xx, zz, cc):
        return (xx * NZ + zz) * 2 + cc

    def at_seq(i):
        return (i, y)

    def remote(src, dst, send, recv, device):
        return pltpu.make_async_remote_copy(
            src_ref=src, dst_ref=dst, send_sem=send, recv_sem=recv,
            device_id=device, device_id_type=pl.DeviceIdType.MESH,
        )

    z_up = seq_id(x, (z + 1) % NZ, c)
    z_down = seq_id(x, (z + NZ - 1) % NZ, c)
    partner = seq_id(x, z, 1 - c)

    def x_peer(d):
        return ((x + d) % NX) * NZC + zc

    barrier = pltpu.get_barrier_semaphore()
    greeted = [((s + seqs - 1) % seqs, y)]
    greeted += [(s, (y + d) % NY) for d in (1, 2, 3)]
    greeted += [(x_peer(d), y) for d in (1, 2, 3)]
    greeted += [(z_up, y), (z_down, y), (partner, y)]
    greeted += [(((x + d) % NX) * NZC + (zc + 1) % NZC, y) for d in range(NX)]
    for device in greeted:
        pl.semaphore_signal(barrier, inc=1, device_id=device, device_id_type=pl.DeviceIdType.MESH)

    tail = 16
    tail_copy = pltpu.make_async_copy(
        tokens.at[pl.ds(rows - tail, tail)], tok.at[pl.ds(rows - tail, tail)], tok_sem.at[0])
    head_copy = pltpu.make_async_copy(
        tokens.at[pl.ds(0, rows - tail)], tok.at[pl.ds(0, rows - tail)], tok_sem.at[1])
    tail_copy.start()
    head_copy.start()
    y_of_slot = [y, (y + 3) % NY, (y + 1) % NY, (y + 2) % NY]
    w_copies = []
    for slot in range(4):
        for j, w in enumerate((w_k, w_v, w_q)):
            rows_w = pl.ds(pl.multiple_of(y_of_slot[slot] * part_width, part_width), part_width)
            cp = pltpu.make_async_copy(w.at[rows_w], weights.at[slot, j], w_sem.at[slot, j])
            cp.start()
            w_copies.append(cp)

    tail_copy.wait()
    for b in range(lane_blocks):
        tok32[b, pl.ds(rows - 8, 16), :] = tok[pl.ds(rows - tail, tail), pl.ds(b * 128, 128)].astype(F32)
    pl.semaphore_wait(barrier, len(greeted))
    bnd = remote(
        tok32.at[:, pl.ds(rows, 8), :], tok32.at[:, pl.ds(0, 8), :],
        bnd_sem.at[0], bnd_sem.at[1], at_seq((s + 1) % seqs))
    bnd.start()
    head_copy.wait()
    for b in range(lane_blocks):
        tok32[b, pl.ds(8, rows - tail), :] = tok[pl.ds(0, rows - tail), pl.ds(b * 128, 128)].astype(F32)
    bnd.wait_recv()

    @pl.when(s == 0)
    def _():
        tok32[:, pl.ds(0, 8), :] = jnp.zeros((lane_blocks, 8, 128), F32)

    part[...] = jnp.zeros_like(part)
    square = jnp.zeros((CD, 128), F32)
    for b in range(lane_blocks):
        lanes = pl.ds(b * 128, 128)
        first = tok32[b, pl.ds(6, CD, stride=3), :]
        second = tok32[b, pl.ds(7, CD, stride=3), :]
        third = tok32[b, pl.ds(8, CD, stride=3), :]
        p = first * w_short[0:1, lanes] + second * w_short[1:2, lanes] + third * w_short[2:3, lanes]
        pooled[b] = p
        square = square + p * p
    part[pl.ds(0, CD), :] = square
    sums[0] = jnp.broadcast_to(jnp.sum(part[...].T, axis=0, keepdims=True), (8, 128))
    ss = []
    for d in (1, 2, 3):
        cp = remote(sums.at[0], sums.at[d], ss_send.at[d - 1], ss_recv.at[d - 1], (s, (y + d) % NY))
        cp.start()
        ss.append(cp)
    for cp in ss:
        cp.wait_recv()
    total = sums[0] + sums[1] + sums[2] + sums[3]
    scale_row = lax.rsqrt(total / width + 1e-05)
    part[...] = jnp.broadcast_to(scale_row[0:1], (128, 128))
    scale = part[...].T[0:CD]
    for b in range(lane_blocks):
        h, o = divmod(b * 128, half)
        coarse[0, h, :, pl.ds(o, 128)] = (pooled[b] * scale).astype(BF16)

    y_up = (s, (y + 1) % NY)
    y_down = (s, (y + 3) % NY)
    sends = []

    def y_copy(src, dst, h, i, device):
        r = (dst - 1) * 2 + h
        return remote(coarse.at[src, h], coarse.at[dst, h], y_send.at[i], y_recv.at[r], device)

    own = [y_copy(0, 1, 0, 0, y_up), y_copy(0, 2, 1, 1, y_down), y_copy(0, 1, 1, 2, y_up), y_copy(0, 2, 0, 3, y_down)]
    for cp in own:
        cp.start()
        sends.append(cp)
    relay = [y_copy(1, 3, 0, 4, y_up), y_copy(2, 3, 1, 5, y_down)]

    def wait_block(slot, h):
        y_copy(slot, slot, h, 0, y_up).wait_recv()

    def project(slot, h, j):
        w = weights[slot, j, pl.ds(h * half, half), :]
        return jnp.dot(coarse[slot, h], w, preferred_element_type=F32)

    def add_block(slot, h):
        for j in range(3):
            acc[j] = acc[j] + project(slot, h, j)

    for j in range(3):
        w_copies[j].wait()
        acc[j] = jnp.dot(coarse[0, 0], weights[0, j, pl.ds(0, half), :], preferred_element_type=F32)
    wait_block(1, 0)
    relay[0].start()
    wait_block(2, 1)
    relay[1].start()
    sends += relay
    add_block(0, 1)
    for cp in w_copies[3:]:
        cp.wait()
    add_block(1, 0)
    add_block(2, 1)
    wait_block(1, 1)
    add_block(1, 1)
    wait_block(2, 0)
    add_block(2, 0)
    wait_block(3, 0)
    add_block(3, 0)
    wait_block(3, 1)

    def x_abs(d):
        return (x + d) % NX

    def block_rows(xx):
        return pl.ds(pl.multiple_of(xx * CD, CD), CD)

    def sub(slot, d):
        return kv.at[slot, :, block_rows(x_abs(d)), :]

    for j in range(2):
        r = (acc[j] + project(3, 1, j)).astype(BF16)
        for h in range(NX):
            kv_out[h, j] = r[:, h * HD:(h + 1) * HD]
    for d in (1, 3, 2):
        cp = remote(
            kv_out.at[x_abs(d)], kv.at[0, :, block_rows(x), :],
            s2_send.at[d - 1], s2_recv.at[NX - d - 1], at_seq(x_peer(d)))
        cp.start()
        sends.append(cp)
    own_kv = kv_out[x]
    kv[0, :, block_rows(x), :] = own_kv

    def ring_copy(up, src_slot, t_next, dst_slot, i, d):
        send = cw_send if up else ccw_send
        recv = cw_recv if up else ccw_recv
        return remote(
            sub(src_slot, d), sub(dst_slot, d), send.at[t_next - 1, i], recv.at[t_next - 1, i],
            at_seq(z_up if up else z_down))

    def partner_copy(slot, i, d):
        return remote(sub(slot, d), sub(NZ + slot, d), pt_send.at[slot, i], pt_recv.at[slot, i], at_seq(partner))

    last = NZ - 1

    def start_ring(i, d):
        for up in (True, False):
            if NT > 1:
                ring_copy(up, 0, 1, 1 if up else NT, i, d).start()
            elif (i < 2) == up:
                ring_copy(up, 0, 1, last, i, d).start()
        partner_copy(0, i, d).start()

    start_ring(0, 0)

    r = (acc[2] + project(3, 1, 2)).astype(BF16)
    for h in range(NX):
        q_out[h] = r[:, h * HD:(h + 1) * HD]
    for d in (1, 3, 2):
        cp = remote(
            q_out.at[x_abs(d)], q_all.at[x], q_send.at[d - 1], q_recv.at[NX - d - 1], at_seq(x_peer(d)))
        cp.start()
        sends.append(cp)
    q_all[x] = q_out[x]

    for i, d in enumerate(DORDER):
        if d:
            remote(sub(0, d), sub(0, d), s2_send.at[0], s2_recv.at[d - 1], at_seq(partner)).wait_recv()
            start_ring(i, d)
    for d in (1, 3, 2):
        remote(q_all.at[x_abs(d)], q_all.at[x_abs(d)], q_send.at[0], q_recv.at[d - 1], at_seq(partner)).wait_recv()

    slope = math.log2(math.e) / math.sqrt(HD)
    for xq in range(NX):
        padded = jnp.concatenate([q_all[xq], jnp.zeros((128 - CD, HD), BF16)], axis=0) if CD < 128 else q_all[xq]
        q_t[:, pl.ds(xq * 128, 128)] = padded.T

    def allow(sc, pair, xk, allowed, first):
        if xk < 2 * pair:
            return sc
        lane = lax.broadcasted_iota(jnp.int32, (CD, 256), 1)
        lower = xk == 2 * pair
        if first:
            row = lax.broadcasted_iota(jnp.int32, (CD, 256), 0)
            ok = (lane >= 128) | (row <= lane) if lower else (lane >= 128) & (row <= lane - 128)
        else:
            ok = lane >= (jnp.where(allowed, 0, 128) if lower else jnp.where(allowed, 128, 256))
        return jnp.where(ok, sc, MASKED)

    def attend(slot, allowed, first=False):
        for pair in range(NX // 2):
            blocks = 2 * pair + 2
            keys = pl.ds(0, blocks * CD)
            lanes = pl.ds(pair * 256, 256)
            sc = jnp.dot(kv[slot, 0, keys, :], q_t[:, lanes], preferred_element_type=F32)
            parts = [allow(sc[k * CD:(k + 1) * CD], pair, k, allowed, first) for k in range(blocks)]
            tops = [jnp.max(p.reshape(CD // 8, 8, 256), axis=0) for p in parts]
            top = jnp.max(functools.reduce(jnp.maximum, tops), axis=0, keepdims=True)
            if not first:
                old = m_s[0:1, lanes]
                top = jnp.maximum(old, top)
                alpha = jnp.exp2((old - top) * slope)
            m_s[:, lanes] = jnp.broadcast_to(top, (8, 256))
            w = [jnp.exp2((p - top) * slope) for p in parts]
            lw = functools.reduce(jnp.add, [jnp.sum(p.reshape(CD // 8, 8, 256), axis=0) for p in w])
            rounded = jnp.concatenate([p.astype(BF16) for p in w], axis=0)
            added = lax.dot_general(
                kv[slot, 1, keys, :], rounded, (((0,), (0,)), ((), ())), preferred_element_type=F32)
            if first:
                l_s[:, lanes] = lw
                o_s[:, lanes] = added
            else:
                l_s[:, lanes] = l_s[:, lanes] * alpha + lw
                o_s[:, lanes] = o_s[:, lanes] * alpha + added

    def wait_partner(slot):
        for i, d in enumerate(DORDER):
            remote(sub(NZ + slot, d), sub(NZ + slot, d), pt_send.at[slot, i], pt_recv.at[slot, i], at_seq(partner)).wait_recv()

    attend(0, None, first=True)
    wait_partner(0)
    attend(NZ, c == 1)

    def arrived(up, t, slot, i, d):
        recv = cw_recv if up else ccw_recv
        send = cw_send if up else ccw_send
        remote(sub(slot, d), sub(slot, d), send.at[t - 1, i], recv.at[t - 1, i], at_seq(partner)).wait_recv()

    def ring_step(t, carry):
        for i, d in enumerate(DORDER):
            for up in (True, False):
                slot = t if up else NT - 1 + t
                arrived(up, t, slot, i, d)

                @pl.when(t + 1 < NT)
                def _():
                    ring_copy(up, slot, t + 1, slot + 1, i, d).start()

                if (i < 2) == up:
                    @pl.when(t + 1 == NT)
                    def _():
                        ring_copy(up, slot, t + 1, last, i, d).start()

                partner_copy(slot, i, d).start()

        def both(k, carry):
            @pl.when(k >= 2)
            def _():
                wait_partner(t + (k % 2) * (NT - 1))

            slot = t + (k % 2) * (NT - 1) + (k // 2) * NZ
            lower = jnp.where(k % 2 == 0, z - t, z + t - NZ) >= 0
            attend(slot, lower)
            return carry

        lax.fori_loop(0, 4, both, 0)
        return carry

    lax.fori_loop(1, NT, ring_step, 0)

    for i, d in enumerate(DORDER):
        arrived(i < 2, NT, last, i, d)
        partner_copy(last, i, d).start()
    lower = z >= NT
    attend(last, lower)
    wait_partner(last)
    attend(NZ + last, lower)

    for xq in range(NX):
        lanes = pl.ds(xq * 128, 128)
        totals = jnp.sum(l_s[:, lanes], axis=0, keepdims=True)
        ctx[xq] = (o_s[:, lanes] / totals).T[0:CD].astype(BF16)
    wrap = jnp.where(zc == 0, 1, 0)
    before = (zc + NZC - 1) % NZC
    for d in (1, 3, 2):
        cp = remote(
            ctx.at[x_abs(d)], win.at[x, pl.ds(0, CD), :], o_send.at[d - 1], o_recv.at[NX - d - 1], at_seq(x_peer(d)))
        cp.start()
        sends.append(cp)
    for d in DORDER:
        target = x_abs(d) * NZC + before
        cp = remote(
            ctx.at[(x + d + wrap) % NX], win.at[x, pl.ds(CD, CD), :], n_send.at[d], n_recv.at[(NX - d) % NX], at_seq(target))
        cp.start()
        sends.append(cp)
    win[x, pl.ds(0, CD), :] = ctx[x]
    for d in (1, 3, 2):
        dst = win.at[x_abs(d), pl.ds(0, CD), :]
        remote(dst, dst, o_send.at[0], o_recv.at[d - 1], at_seq(partner)).wait_recv()
    for d in DORDER:
        dst = win.at[x_abs(d), pl.ds(CD, CD), :]
        remote(dst, dst, n_send.at[0], n_recv.at[d], at_seq(partner)).wait_recv()

    lane = lax.broadcasted_iota(jnp.int32, (1, seqs), 1)
    lens = lengths[...]
    start = jnp.sum(jnp.where(lane < s, lens, 0), axis=1, keepdims=True) - s * CD
    count = jnp.sum(jnp.where(lane == s, lens, 0), axis=1, keepdims=True)
    row = lax.broadcasted_iota(jnp.int32, (2 * CD, 2 * CD), 0)
    col = lax.broadcasted_iota(jnp.int32, (2 * CD, 2 * CD), 1)
    pick = jnp.where((col == row + start) & (row < count), 1.0, 0.0).astype(BF16)
    for h in range(NX):
        out[:, pl.ds(h * HD, HD)] = jnp.dot(pick, win[h], preferred_element_type=F32).astype(BF16)

    bnd.wait_send()
    for cp in ss + sends:
        cp.wait_send()
    for i, d in enumerate(DORDER):
        def sent(t, carry):
            for up in (True, False):
                ring_copy(up, 0, t, 0, i, d).wait_send()
            return carry

        lax.fori_loop(1, NT, sent, 0)
        ring_copy(i < 2, 0, NT, 0, i, d).wait_send()

        def passed(slot, carry):
            partner_copy(slot, i, d).wait_send()
            return carry

        lax.fori_loop(0, NZ, passed, 0)


def shards(seqs, tokens, w_short, w_query, w_key, w_value, owner_lengths):
    rows, part_width = tokens.shape
    CD = rows // 3
    width = part_width * NY
    features = w_query.shape[1]
    NZ = seqs // (2 * NX)
    NT = NZ // 2
    half = part_width // 2
    dma = pltpu.SemaphoreType.DMA
    vmem = pl.BlockSpec(memory_space=pltpu.VMEM)
    hbm = pl.BlockSpec(memory_space=pl.ANY)
    return pl.pallas_call(
        functools.partial(layer_kernel, seqs, width),
        out_shape=jax.ShapeDtypeStruct((2 * CD, features), BF16),
        in_specs=[hbm, vmem, hbm, hbm, hbm, vmem],
        out_specs=vmem,
        scratch_shapes=[
            pltpu.VMEM((rows, part_width), BF16),
            pltpu.VMEM((part_width // 128, rows + 8, 128), F32),
            pltpu.VMEM((part_width // 128, CD, 128), F32),
            pltpu.VMEM((128, 128), F32),
            pltpu.VMEM((4, 8, 128), F32),
            pltpu.VMEM((4, 2, CD, half), BF16),
            pltpu.VMEM((4, 3, part_width, features), BF16),
            pltpu.VMEM((3, CD, features), F32),
            pltpu.VMEM((NX, 2, CD, HD), BF16),
            pltpu.VMEM((NX, CD, HD), BF16),
            pltpu.VMEM((2 * NZ, 2, NX * CD, HD), BF16),
            pltpu.VMEM((NX, CD, HD), BF16),
            pltpu.VMEM((HD, NX * 128), BF16),
            pltpu.VMEM((8, NX * 128), F32),
            pltpu.VMEM((8, NX * 128), F32),
            pltpu.VMEM((HD, NX * 128), F32),
            pltpu.VMEM((NX, CD, HD), BF16),
            pltpu.VMEM((NX, 2 * CD, HD), BF16),
            dma((2,)), dma((4, 3)), dma((2,)), dma((3,)), dma((3,)), dma((6,)), dma((6,)),
            dma((3,)), dma((3,)), dma((3,)), dma((3,)),
            dma((NT, 4)), dma((NT, 4)), dma((NT, 4)), dma((NT, 4)),
            dma((NZ, 4)), dma((NZ, 4)), dma((3,)), dma((3,)), dma((4,)), dma((4,)),
        ],
        compiler_params=pltpu.CompilerParams(
            collective_id=0, has_side_effects=True, vmem_limit_bytes=56 * 1024 * 1024),
        name="layer",
    )(tokens, w_short, w_query, w_key, w_value, owner_lengths.reshape(1, seqs))


def solution(mesh):
    return jax.shard_map(
        functools.partial(shards, mesh.shape["seq"]),
        mesh=mesh,
        in_specs=(
            P("seq", "head"),
            P(None, "head"),
            P(None, "head"),
            P(None, "head"),
            P(None, "head"),
            P(),
        ),
        out_specs=P("seq", "head"),
        check_vma=False,
    )
```

```python
import functools
import math

import jax
import jax.numpy as jnp
from jax import lax
from jax.experimental import pallas as pl
from jax.experimental.pallas import tpu as pltpu
from jax.sharding import PartitionSpec as P

HD = 128
NX = 4
NY = 4
MASKED = -1e30
F32 = jnp.float32
BF16 = jnp.bfloat16
DORDER = (0, 1, 3, 2)


def layer_kernel(
    seqs, width,
    tokens, w_short_hbm, w_q, w_k, w_v, lengths_hbm,
    out,
    w_short, lengths, tok, tok32, pooled, part, sums, coarse, weights, acc, kv_out, q_out, kv, q_all,
    q_t, m_s, l_s, o_s, ctx, win,
    tok_sem, w_sem, bnd_sem, ss_send, ss_recv, y_send, y_recv,
    s2_send, s2_recv, q_send, q_recv, cw_send, cw_recv, ccw_send, ccw_recv,
    pt_send, pt_recv, o_send, o_recv, n_send, n_recv,
):
    NZ = seqs // (2 * NX)
    NT = NZ // 2
    NZC = 2 * NZ
    rows, part_width = tok.shape
    CD = rows // 3
    lane_blocks = part_width // 128
    half = part_width // 2
    features = NX * HD

    s = lax.axis_index("seq")
    y = lax.axis_index("head")
    x = s // NZC
    zc = s % NZC
    z = zc // 2
    c = zc % 2

    def seq_id(xx, zz, cc):
        return (xx * NZ + zz) * 2 + cc

    def at_seq(i):
        return (i, y)

    def remote(src, dst, send, recv, device):
        return pltpu.make_async_remote_copy(
            src_ref=src, dst_ref=dst, send_sem=send, recv_sem=recv,
            device_id=device, device_id_type=pl.DeviceIdType.MESH,
        )

    z_up = seq_id(x, (z + 1) % NZ, c)
    z_down = seq_id(x, (z + NZ - 1) % NZ, c)
    partner = seq_id(x, z, 1 - c)

    def x_peer(d):
        return ((x + d) % NX) * NZC + zc

    barrier = pltpu.get_barrier_semaphore()
    greeted = [((s + seqs - 1) % seqs, y)]
    greeted += [(s, (y + d) % NY) for d in (1, 2, 3)]
    greeted += [(x_peer(d), y) for d in (1, 2, 3)]
    greeted += [(z_up, y), (z_down, y), (partner, y)]
    greeted += [(((x + d) % NX) * NZC + (zc + 1) % NZC, y) for d in range(NX)]
    for device in greeted:
        pl.semaphore_signal(barrier, inc=1, device_id=device, device_id_type=pl.DeviceIdType.MESH)

    tail = 16
    tail_copy = pltpu.make_async_copy(
        tokens.at[pl.ds(rows - tail, tail)], tok.at[pl.ds(rows - tail, tail)], tok_sem.at[0])
    head_copy = pltpu.make_async_copy(
        tokens.at[pl.ds(0, rows - tail)], tok.at[pl.ds(0, rows - tail)], tok_sem.at[1])
    short_copy = pltpu.make_async_copy(w_short_hbm, w_short, tok_sem.at[2])
    lengths_copy = pltpu.make_async_copy(lengths_hbm, lengths, tok_sem.at[3])
    for cp in (tail_copy, head_copy, short_copy, lengths_copy):
        cp.start()
    y_of_slot = [y, (y + 3) % NY, (y + 1) % NY, (y + 2) % NY]
    w_copies = []
    for slot in range(4):
        for j, w in enumerate((w_k, w_v, w_q)):
            rows_w = pl.ds(pl.multiple_of(y_of_slot[slot] * part_width, part_width), part_width)
            cp = pltpu.make_async_copy(w.at[rows_w], weights.at[slot, j], w_sem.at[slot, j])
            cp.start()
            w_copies.append(cp)

    tail_copy.wait()
    for b in range(lane_blocks):
        tok32[b, pl.ds(rows - 8, 16), :] = tok[pl.ds(rows - tail, tail), pl.ds(b * 128, 128)].astype(F32)
    pl.semaphore_wait(barrier, len(greeted))
    bnd = remote(
        tok32.at[:, pl.ds(rows, 8), :], tok32.at[:, pl.ds(0, 8), :],
        bnd_sem.at[0], bnd_sem.at[1], at_seq((s + 1) % seqs))
    bnd.start()
    head_copy.wait()
    for b in range(lane_blocks):
        tok32[b, pl.ds(8, rows - tail), :] = tok[pl.ds(0, rows - tail), pl.ds(b * 128, 128)].astype(F32)
    bnd.wait_recv()

    @pl.when(s == 0)
    def _():
        tok32[:, pl.ds(0, 8), :] = jnp.zeros((lane_blocks, 8, 128), F32)

    short_copy.wait()
    part[...] = jnp.zeros_like(part)
    square = jnp.zeros((CD, 128), F32)
    for b in range(lane_blocks):
        lanes = pl.ds(b * 128, 128)
        first = tok32[b, pl.ds(6, CD, stride=3), :]
        second = tok32[b, pl.ds(7, CD, stride=3), :]
        third = tok32[b, pl.ds(8, CD, stride=3), :]
        p = first * w_short[0:1, lanes] + second * w_short[1:2, lanes] + third * w_short[2:3, lanes]
        pooled[b] = p
        square = square + p * p
    part[pl.ds(0, CD), :] = square
    sums[0] = jnp.broadcast_to(jnp.sum(part[...].T, axis=0, keepdims=True), (8, 128))
    ss = []
    for d in (1, 2, 3):
        cp = remote(sums.at[0], sums.at[d], ss_send.at[d - 1], ss_recv.at[d - 1], (s, (y + d) % NY))
        cp.start()
        ss.append(cp)
    for cp in ss:
        cp.wait_recv()
    total = sums[0] + sums[1] + sums[2] + sums[3]
    scale_row = lax.rsqrt(total / width + 1e-05)
    part[...] = jnp.broadcast_to(scale_row[0:1], (128, 128))
    scale = part[...].T[0:CD]
    for b in range(lane_blocks):
        h, o = divmod(b * 128, half)
        coarse[0, h, :, pl.ds(o, 128)] = (pooled[b] * scale).astype(BF16)

    y_up = (s, (y + 1) % NY)
    y_down = (s, (y + 3) % NY)
    sends = []

    def y_copy(src, dst, h, i, device):
        r = (dst - 1) * 2 + h
        return remote(coarse.at[src, h], coarse.at[dst, h], y_send.at[i], y_recv.at[r], device)

    own = [y_copy(0, 1, 0, 0, y_up), y_copy(0, 2, 1, 1, y_down), y_copy(0, 1, 1, 2, y_up), y_copy(0, 2, 0, 3, y_down)]
    for cp in own:
        cp.start()
        sends.append(cp)
    relay = [y_copy(1, 3, 0, 4, y_up), y_copy(2, 3, 1, 5, y_down)]

    def wait_block(slot, h):
        y_copy(slot, slot, h, 0, y_up).wait_recv()

    def project(slot, h, j):
        w = weights[slot, j, pl.ds(h * half, half), :]
        return jnp.dot(coarse[slot, h], w, preferred_element_type=F32)

    def add_block(slot, h):
        for j in range(3):
            acc[j] = acc[j] + project(slot, h, j)

    for j in range(3):
        w_copies[j].wait()
        acc[j] = jnp.dot(coarse[0, 0], weights[0, j, pl.ds(0, half), :], preferred_element_type=F32)
    wait_block(1, 0)
    relay[0].start()
    wait_block(2, 1)
    relay[1].start()
    sends += relay
    add_block(0, 1)
    for cp in w_copies[3:]:
        cp.wait()
    add_block(1, 0)
    add_block(2, 1)
    wait_block(1, 1)
    add_block(1, 1)
    wait_block(2, 0)
    add_block(2, 0)
    wait_block(3, 0)
    add_block(3, 0)
    wait_block(3, 1)

    def x_abs(d):
        return (x + d) % NX

    def block_rows(xx):
        return pl.ds(pl.multiple_of(xx * CD, CD), CD)

    def sub(slot, d):
        return kv.at[slot, :, block_rows(x_abs(d)), :]

    for j in range(2):
        r = (acc[j] + project(3, 1, j)).astype(BF16)
        for h in range(NX):
            kv_out[h, j] = r[:, h * HD:(h + 1) * HD]
    for d in (1, 3, 2):
        cp = remote(
            kv_out.at[x_abs(d)], kv.at[0, :, block_rows(x), :],
            s2_send.at[d - 1], s2_recv.at[NX - d - 1], at_seq(x_peer(d)))
        cp.start()
        sends.append(cp)
    own_kv = kv_out[x]
    kv[0, :, block_rows(x), :] = own_kv

    def ring_copy(up, src_slot, t_next, dst_slot, i, d):
        send = cw_send if up else ccw_send
        recv = cw_recv if up else ccw_recv
        return remote(
            sub(src_slot, d), sub(dst_slot, d), send.at[t_next - 1, i], recv.at[t_next - 1, i],
            at_seq(z_up if up else z_down))

    def partner_copy(slot, i, d):
        return remote(sub(slot, d), sub(NZ + slot, d), pt_send.at[slot, i], pt_recv.at[slot, i], at_seq(partner))

    last = NZ - 1

    def start_ring(i, d):
        for up in (True, False):
            if NT > 1:
                ring_copy(up, 0, 1, 1 if up else NT, i, d).start()
            elif (i < 2) == up:
                ring_copy(up, 0, 1, last, i, d).start()
        partner_copy(0, i, d).start()

    start_ring(0, 0)

    r = (acc[2] + project(3, 1, 2)).astype(BF16)
    for h in range(NX):
        q_out[h] = r[:, h * HD:(h + 1) * HD]
    for d in (1, 3, 2):
        cp = remote(
            q_out.at[x_abs(d)], q_all.at[x], q_send.at[d - 1], q_recv.at[NX - d - 1], at_seq(x_peer(d)))
        cp.start()
        sends.append(cp)
    q_all[x] = q_out[x]

    for i, d in enumerate(DORDER):
        if d:
            remote(sub(0, d), sub(0, d), s2_send.at[0], s2_recv.at[d - 1], at_seq(partner)).wait_recv()
            start_ring(i, d)
    for d in (1, 3, 2):
        remote(q_all.at[x_abs(d)], q_all.at[x_abs(d)], q_send.at[0], q_recv.at[d - 1], at_seq(partner)).wait_recv()

    slope = math.log2(math.e) / math.sqrt(HD)
    for xq in range(NX):
        padded = jnp.concatenate([q_all[xq], jnp.zeros((128 - CD, HD), BF16)], axis=0) if CD < 128 else q_all[xq]
        q_t[:, pl.ds(xq * 128, 128)] = padded.T

    def allow(sc, pair, xk, allowed, first):
        if xk < 2 * pair:
            return sc
        lane = lax.broadcasted_iota(jnp.int32, (CD, 256), 1)
        lower = xk == 2 * pair
        if first:
            row = lax.broadcasted_iota(jnp.int32, (CD, 256), 0)
            ok = (lane >= 128) | (row <= lane) if lower else (lane >= 128) & (row <= lane - 128)
        else:
            ok = lane >= (jnp.where(allowed, 0, 128) if lower else jnp.where(allowed, 128, 256))
        return jnp.where(ok, sc, MASKED)

    def attend(slot, allowed, first=False):
        for pair in range(NX // 2):
            blocks = 2 * pair + 2
            keys = pl.ds(0, blocks * CD)
            lanes = pl.ds(pair * 256, 256)
            sc = jnp.dot(kv[slot, 0, keys, :], q_t[:, lanes], preferred_element_type=F32)
            parts = [allow(sc[k * CD:(k + 1) * CD], pair, k, allowed, first) for k in range(blocks)]
            tops = [jnp.max(p.reshape(CD // 8, 8, 256), axis=0) for p in parts]
            top = jnp.max(functools.reduce(jnp.maximum, tops), axis=0, keepdims=True)
            if not first:
                old = m_s[0:1, lanes]
                top = jnp.maximum(old, top)
                alpha = jnp.exp2((old - top) * slope)
            m_s[:, lanes] = jnp.broadcast_to(top, (8, 256))
            w = [jnp.exp2((p - top) * slope) for p in parts]
            lw = functools.reduce(jnp.add, [jnp.sum(p.reshape(CD // 8, 8, 256), axis=0) for p in w])
            rounded = jnp.concatenate([p.astype(BF16) for p in w], axis=0)
            added = lax.dot_general(
                kv[slot, 1, keys, :], rounded, (((0,), (0,)), ((), ())), preferred_element_type=F32)
            if first:
                l_s[:, lanes] = lw
                o_s[:, lanes] = added
            else:
                l_s[:, lanes] = l_s[:, lanes] * alpha + lw
                o_s[:, lanes] = o_s[:, lanes] * alpha + added

    def wait_partner(slot):
        for i, d in enumerate(DORDER):
            remote(sub(NZ + slot, d), sub(NZ + slot, d), pt_send.at[slot, i], pt_recv.at[slot, i], at_seq(partner)).wait_recv()

    attend(0, None, first=True)
    wait_partner(0)
    attend(NZ, c == 1)

    def arrived(up, t, slot, i, d):
        recv = cw_recv if up else ccw_recv
        send = cw_send if up else ccw_send
        remote(sub(slot, d), sub(slot, d), send.at[t - 1, i], recv.at[t - 1, i], at_seq(partner)).wait_recv()

    def ring_step(t, carry):
        for i, d in enumerate(DORDER):
            for up in (True, False):
                slot = t if up else NT - 1 + t
                arrived(up, t, slot, i, d)

                @pl.when(t + 1 < NT)
                def _():
                    ring_copy(up, slot, t + 1, slot + 1, i, d).start()

                if (i < 2) == up:
                    @pl.when(t + 1 == NT)
                    def _():
                        ring_copy(up, slot, t + 1, last, i, d).start()

                partner_copy(slot, i, d).start()

        def both(k, carry):
            @pl.when(k >= 2)
            def _():
                wait_partner(t + (k % 2) * (NT - 1))

            slot = t + (k % 2) * (NT - 1) + (k // 2) * NZ
            lower = jnp.where(k % 2 == 0, z - t, z + t - NZ) >= 0
            attend(slot, lower)
            return carry

        lax.fori_loop(0, 4, both, 0)
        return carry

    lax.fori_loop(1, NT, ring_step, 0)

    for i, d in enumerate(DORDER):
        arrived(i < 2, NT, last, i, d)
        partner_copy(last, i, d).start()
    lower = z >= NT
    attend(last, lower)
    wait_partner(last)
    attend(NZ + last, lower)

    for xq in range(NX):
        lanes = pl.ds(xq * 128, 128)
        totals = jnp.sum(l_s[:, lanes], axis=0, keepdims=True)
        ctx[xq] = (o_s[:, lanes] / totals).T[0:CD].astype(BF16)
    wrap = jnp.where(zc == 0, 1, 0)
    before = (zc + NZC - 1) % NZC
    for d in (1, 3, 2):
        cp = remote(
            ctx.at[x_abs(d)], win.at[x, pl.ds(0, CD), :], o_send.at[d - 1], o_recv.at[NX - d - 1], at_seq(x_peer(d)))
        cp.start()
        sends.append(cp)
    for d in DORDER:
        target = x_abs(d) * NZC + before
        cp = remote(
            ctx.at[(x + d + wrap) % NX], win.at[x, pl.ds(CD, CD), :], n_send.at[d], n_recv.at[(NX - d) % NX], at_seq(target))
        cp.start()
        sends.append(cp)
    win[x, pl.ds(0, CD), :] = ctx[x]
    for d in (1, 3, 2):
        dst = win.at[x_abs(d), pl.ds(0, CD), :]
        remote(dst, dst, o_send.at[0], o_recv.at[d - 1], at_seq(partner)).wait_recv()
    for d in DORDER:
        dst = win.at[x_abs(d), pl.ds(CD, CD), :]
        remote(dst, dst, n_send.at[0], n_recv.at[d], at_seq(partner)).wait_recv()

    lane = lax.broadcasted_iota(jnp.int32, (1, seqs), 1)
    lengths_copy.wait()
    lens = lengths[...]
    start = jnp.sum(jnp.where(lane < s, lens, 0), axis=1, keepdims=True) - s * CD
    count = jnp.sum(jnp.where(lane == s, lens, 0), axis=1, keepdims=True)
    row = lax.broadcasted_iota(jnp.int32, (2 * CD, 2 * CD), 0)
    col = lax.broadcasted_iota(jnp.int32, (2 * CD, 2 * CD), 1)
    pick = jnp.where((col == row + start) & (row < count), 1.0, 0.0).astype(BF16)
    for h in range(NX):
        out[:, pl.ds(h * HD, HD)] = jnp.dot(pick, win[h], preferred_element_type=F32).astype(BF16)

    bnd.wait_send()
    for cp in ss + sends:
        cp.wait_send()
    for i, d in enumerate(DORDER):
        def sent(t, carry):
            for up in (True, False):
                ring_copy(up, 0, t, 0, i, d).wait_send()
            return carry

        lax.fori_loop(1, NT, sent, 0)
        ring_copy(i < 2, 0, NT, 0, i, d).wait_send()

        def passed(slot, carry):
            partner_copy(slot, i, d).wait_send()
            return carry

        lax.fori_loop(0, NZ, passed, 0)


def shards(seqs, tokens, w_short, w_query, w_key, w_value, owner_lengths):
    rows, part_width = tokens.shape
    CD = rows // 3
    width = part_width * NY
    features = w_query.shape[1]
    NZ = seqs // (2 * NX)
    NT = NZ // 2
    half = part_width // 2
    dma = pltpu.SemaphoreType.DMA
    vmem = pl.BlockSpec(memory_space=pltpu.VMEM)
    hbm = pl.BlockSpec(memory_space=pl.ANY)
    return pl.pallas_call(
        functools.partial(layer_kernel, seqs, width),
        out_shape=pltpu.VMEM((2 * CD, features), BF16),
        in_specs=[hbm, hbm, hbm, hbm, hbm, hbm],
        out_specs=vmem,
        scratch_shapes=[
            pltpu.VMEM((3, part_width), F32),
            pltpu.VMEM((1, seqs), jnp.int32),
            pltpu.VMEM((rows, part_width), BF16),
            pltpu.VMEM((part_width // 128, rows + 8, 128), F32),
            pltpu.VMEM((part_width // 128, CD, 128), F32),
            pltpu.VMEM((128, 128), F32),
            pltpu.VMEM((4, 8, 128), F32),
            pltpu.VMEM((4, 2, CD, half), BF16),
            pltpu.VMEM((4, 3, part_width, features), BF16),
            pltpu.VMEM((3, CD, features), F32),
            pltpu.VMEM((NX, 2, CD, HD), BF16),
            pltpu.VMEM((NX, CD, HD), BF16),
            pltpu.VMEM((2 * NZ, 2, NX * CD, HD), BF16),
            pltpu.VMEM((NX, CD, HD), BF16),
            pltpu.VMEM((HD, NX * 128), BF16),
            pltpu.VMEM((8, NX * 128), F32),
            pltpu.VMEM((8, NX * 128), F32),
            pltpu.VMEM((HD, NX * 128), F32),
            pltpu.VMEM((NX, CD, HD), BF16),
            pltpu.VMEM((NX, 2 * CD, HD), BF16),
            dma((4,)), dma((4, 3)), dma((2,)), dma((3,)), dma((3,)), dma((6,)), dma((6,)),
            dma((3,)), dma((3,)), dma((3,)), dma((3,)),
            dma((NT, 4)), dma((NT, 4)), dma((NT, 4)), dma((NT, 4)),
            dma((NZ, 4)), dma((NZ, 4)), dma((3,)), dma((3,)), dma((4,)), dma((4,)),
        ],
        compiler_params=pltpu.CompilerParams(
            collective_id=0, has_side_effects=True, vmem_limit_bytes=56 * 1024 * 1024),
        name="layer",
    )(tokens, w_short, w_query, w_key, w_value, owner_lengths.reshape(1, seqs))


def solution(mesh):
    return jax.shard_map(
        functools.partial(shards, mesh.shape["seq"]),
        mesh=mesh,
        in_specs=(
            P("seq", "head"),
            P(None, "head"),
            P(None, "head"),
            P(None, "head"),
            P(None, "head"),
            P(),
        ),
        out_specs=P("seq", "head"),
        check_vma=False,
    )
```
